32 devices in a mesh: comp: 4 (over y, x), dom: 8 (over z, core).
Axes of the slice: x: 2, y: 2, z: 4, core: 2. Of those that a mesh axis runs over, the one named last changes fastest.
Arguments:
- state: float32 [72, 524288], P(None, ('comp', 'dom')), may hold values from -6 to 6
- forcing: float32 [8, 524288], P(None, ('comp', 'dom')), may hold values from -6 to 6
- vertical: float32 [4, 72, 72], P('comp'), may hold values from -0.75 to 0.75
- inject: float32 [4, 72, 8], P('comp'), may hold values from -2 to 2
- extract: float32 [4, 8, 72], P('comp'), may hold values from -0.75 to 0.75
- diffuse: float32 [524288], P(('comp', 'dom')), may hold values from 0.05 to 0.24
- substeps: int32 [524288], P(('comp', 'dom')), may hold values from 1 to 4, as said below
- landmask: int32 [524288], P(('comp', 'dom')), may hold values 0 or 1
- links: int32 [3, 32, 32, 2], P(None, ('comp', 'dom')), may hold values from -1 to 127, as said below
- remap_weight_matrices: float32 [512, 128, 128], P(('comp', 'dom')), may hold values from -0.5 to 0.5
Outputs:
- state_next: float32 [72, 524288], P(None, ('comp', 'dom'))
- forcing_next: float32 [8, 524288], P(None, ('comp', 'dom'))
The draws below stay inside these ranges and needn't reach their ends.
Inputs may be any that keep to these rules, and one draw needn't show every extreme that they name: substeps holds each column's count of substeps; 4 and 1 occur in every draw. In each [g, h, k] either all three fields are -1 (an empty slot) or links[0] and links[1] are blocks 0 to 127 and links[2] a slot 0 to 15; live slots of a pair come first; live entries join an atmosphere device (index below (3) * 8) with an ocean device only, and every such pair has one or more live slots; a pair has at most 2 live slots, and some pair reaches 2 in every draw.
All inputs are finite; a program needn't handle non-finite values. No bound on the sum of `landmask` on one device may be relied on, other than what follows from the above.
Results may differ from the reference program's by a relative error of at most 0.0003.
Values sent between devices are 32-bit elements; how exact they have to be, the bound alone decides.
A program may use at most 128 MiB of HBM per device.

```python
import math
import jax
import jax.numpy as jnp
from jax import lax

LEV = 72
NF = 8
INTERSECT_WIDTH = 128
NB = 128
SLOTS_PER_TARGET = 2
WEIGHT_SLOTS = 16
SUBS = 4
SECTIONS = 4
CELLS = 524288
N_COMP = 4
N_DOM = 8


def draw_substeps(key, part):
    counts = jax.random.randint(key, (N_COMP * N_DOM * NB * INTERSECT_WIDTH,), 1, SUBS + 1)
    return counts.at[0].set(SUBS).at[1].set(1).astype(jnp.int32)


def draw_links(key, part):
    every_device_list = N_COMP * N_DOM
    atmos_count = (N_COMP - 1) * N_DOM
    random_subkeys = jax.random.split(jax.random.fold_in(key, 11), 5)
    is_atmos = jnp.arange(every_device_list) < atmos_count
    partner = (is_atmos[:, None] != is_atmos[None, :]).astype(jnp.int32)
    fuller = jax.random.randint(random_subkeys[0], (every_device_list, every_device_list), 0, 4)
    live_count = jnp.where(fuller > 0, SLOTS_PER_TARGET, jnp.maximum(SLOTS_PER_TARGET - 1, 1)) * partner
    live_count = live_count.at[0, atmos_count].set(SLOTS_PER_TARGET).at[atmos_count, 0].set(SLOTS_PER_TARGET)
    is_live = jnp.arange(SLOTS_PER_TARGET)[None, None, :] < live_count[:, :, None]
    source_block = jax.random.randint(random_subkeys[2], (every_device_list, every_device_list, SLOTS_PER_TARGET), 0, NB)
    target_block = jax.random.randint(random_subkeys[3], (every_device_list, every_device_list, SLOTS_PER_TARGET), 0, NB)
    matrix_slot_index = jax.random.randint(random_subkeys[4], (every_device_list, every_device_list, SLOTS_PER_TARGET), 0, WEIGHT_SLOTS)
    stacked = jnp.stack([source_block, target_block, matrix_slot_index])
    return jnp.where(is_live[None], stacked, -1).astype(jnp.int32)


def set_ends(array, stream_key, least, largest):
    shape = array.shape
    spot = [jax.random.randint(jax.random.fold_in(stream_key, axis), (), 0, shape[axis]) for axis in range(len(shape))]
    array = array.at[tuple(spot)].set(least)
    longest = shape.index(max(shape))
    spot[longest] = (spot[longest] + 1) % shape[longest]
    return array.at[tuple(spot)].set(largest)


def shard_levels(key, extent, pieces, low, high):
    loudness, own = 1.0, jax.random.fold_in(key, 6)
    for dim, parts in pieces:
        draws = jnp.exp(jax.random.uniform(jax.random.fold_in(own, dim), (parts,), jnp.float32, low / len(pieces), high / len(pieces)))
        loudness = loudness * jnp.repeat(draws, extent[dim] // parts).reshape([-1 if axis == dim else 1 for axis in range(len(extent))])
    return loudness


def normal_values(key, extent, width, bound, cuts=(), kind=jnp.bfloat16):
    entries = jax.random.normal(key, extent, jnp.float32) * width
    if len(cuts) > 0:
        entries = shard_levels(key, extent, cuts, -0.22, 0.18) * entries
    return jnp.clip(entries, min=-bound, max=bound).astype(kind)


def setup_inputs(seed: int = 0) -> dict:
    key_list = jax.random.split(jax.random.key(seed), 11)
    state = normal_values(key_list[0], (LEV, CELLS), 1.0, 6.0, ((1, 32),), jnp.float32)
    forcing = normal_values(key_list[1], (NF, CELLS), 1.0, 6.0, ((1, 32),), jnp.float32)
    vertical = normal_values(key_list[2], (SECTIONS, LEV, LEV), LEV ** -0.5, 0.75, ((0, 4),), jnp.float32)
    inject = normal_values(key_list[3], (SECTIONS, LEV, NF), NF ** -0.5, 2.0, ((0, 4),), jnp.float32)
    extract = normal_values(key_list[4], (SECTIONS, NF, LEV), LEV ** -0.5, 0.75, ((0, 4),), jnp.float32)
    diffuse = jnp.clip(jnp.exp(math.log(0.24) - 1.5686159 * jax.random.uniform(key_list[5], (CELLS,), jnp.float32) ** shard_levels(key_list[5], (CELLS,), ((0, 32),), -0.2, 0.2)), 0.05, 0.24)
    substeps = draw_substeps(jax.random.fold_in(key_list[10], 71), 0)
    landmask = set_ends((jax.random.randint(key_list[7], (CELLS,), 0, 4) < 3).astype(jnp.int32), jax.random.fold_in(key_list[7], 1), 0, 1)
    links = draw_links(jax.random.fold_in(key_list[10], 71), 0)
    remap_weight_matrices = normal_values(key_list[9], (N_COMP * N_DOM * WEIGHT_SLOTS, INTERSECT_WIDTH, INTERSECT_WIDTH), INTERSECT_WIDTH ** -0.5, 0.5, ((0, 32),), jnp.float32)
    return dict(state=state, forcing=forcing, vertical=vertical, inject=inject, extract=extract, diffuse=diffuse, substeps=substeps, landmask=landmask, links=links, remap_weight_matrices=remap_weight_matrices)


DT = 0.25


def reference(state, forcing, vertical, inject, extract, diffuse, substeps, landmask, links, remap_weight_matrices):
    highest = lax.Precision.HIGHEST
    every_device_list = N_COMP * N_DOM
    cycle_len = N_DOM * NB * INTERSECT_WIDTH
    wet_cells = landmask.astype(jnp.float32).reshape(1, N_COMP, cycle_len)
    field = state.reshape(LEV, N_COMP, cycle_len)
    coupled = jnp.einsum("sfl,lsc->fsc", extract, field, precision=highest) * wet_cells
    blocks = coupled.reshape(NF, every_device_list, NB, INTERSECT_WIDTH).transpose(1, 2, 0, 3)
    weight_entries = remap_weight_matrices.reshape(every_device_list, WEIGHT_SLOTS, INTERSECT_WIDTH, INTERSECT_WIDTH)
    tables = links.transpose(1, 0, 2, 3)
    offsets = (jnp.arange(every_device_list, dtype=jnp.int32) * NB)[:, None]

    def add_source(accumulated, entry):
        source_rows, source_weights, device_link_table = entry
        source_block = jnp.clip(device_link_table[0], 0, NB - 1).reshape(-1).astype(jnp.int32)
        target_block = (offsets + jnp.clip(device_link_table[1], 0, NB - 1)).reshape(-1).astype(jnp.int32)
        matrix_slot_index = jnp.clip(device_link_table[2], 0, WEIGHT_SLOTS - 1).reshape(-1).astype(jnp.int32)
        is_live = (device_link_table[0] >= 0).reshape(-1)
        message = jnp.einsum("efb,ebc->efc", source_rows[source_block], source_weights[matrix_slot_index], precision=highest)
        message = jnp.where(is_live[:, None, None], message, jnp.zeros_like(message))
        return accumulated.at[target_block].add(message), None

    start = jnp.zeros((every_device_list * NB, NF, INTERSECT_WIDTH), jnp.float32)
    accumulated, unused = lax.scan(add_source, start, (blocks, weight_entries, tables))
    forcing_next = accumulated.reshape(every_device_list, NB, NF, INTERSECT_WIDTH).transpose(2, 0, 1, 3).reshape(NF, every_device_list * NB * INTERSECT_WIDTH)

    forcing_term = jnp.einsum("slf,fsc->lsc", inject, forcing.reshape(NF, N_COMP, cycle_len), precision=highest) * wet_cells * DT
    mixing = diffuse.reshape(1, N_COMP, cycle_len)
    counts = substeps.reshape(1, N_COMP, cycle_len)
    for substep in range(SUBS):
        spread_term = jnp.roll(field, 1, axis=2) + jnp.roll(field, -1, axis=2) - 2.0 * field
        tendency = jnp.einsum("slm,msc->lsc", vertical, field, precision=highest)
        updated = field + mixing * spread_term + DT * tendency + forcing_term
        field = jnp.where(counts > substep, updated, field)
    return field.reshape(LEV, N_COMP * cycle_len), forcing_next
```

```python
import functools

import jax
import jax.numpy as jnp
from jax import lax
from jax.experimental import pallas as pl
from jax.experimental.pallas import tpu as pltpu
from jax.sharding import PartitionSpec as P

SUBS = 4
DT = 0.25
LANES = 128
WIDE = 256
LEAD = 512
GROUP = 8
CHUNK = 8
PAD_ROWS = 80
MESH = pl.DeviceIdType.MESH
F32 = jnp.float32
BF16 = jnp.bfloat16


def high_low(x):
    high = x.astype(BF16)
    return high, (x - high.astype(F32)).astype(BF16)


def stack_left(matrix, scratch, width):
    high = matrix.astype(BF16).astype(F32)
    low = matrix - high
    scratch[...] = jnp.zeros_like(scratch)
    size = matrix.shape[1]
    scratch[:, 0:size] = high
    scratch[:, width : width + size] = high
    scratch[:, 2 * width : 2 * width + size] = low


def exchange_kernel(
    comps,
    doms,
    links,
    state,
    forcing,
    extract,
    diffuse,
    substeps,
    landmask,
    weights,
    arrived,
    targets,
    halo,
    state_v,
    rows_v,
    edge_f,
    weights_v,
    split_w,
    left_f,
    msg,
    tgt,
    edge,
    state_sem,
    load_sem,
    edge_sem,
    msg_send,
    msg_recv,
    tgt_send,
    tgt_recv,
    halo_send,
    halo_recv,
):
    levels, columns = state.shape
    comp = lax.axis_index("comp")
    dom = lax.axis_index("dom")
    me = comp * doms + dom
    air = (comps - 1) * doms
    is_air = comp < comps - 1
    count = jnp.where(is_air, doms, air)
    first = jnp.where(is_air, air, 0)
    right = lax.rem(dom + 1, doms)
    left = lax.rem(dom + doms - 1, doms)

    span = CHUNK * WIDE
    pieces = columns // span

    def load(c):
        here = pl.ds(pl.multiple_of(c * span, span), span)
        return pltpu.make_async_copy(state.at[:, here], state_v.at[:, here], state_sem.at[c])

    load(pieces - 1).start()
    for c in range(pieces - 1):
        load(c).start()
    load_weights = pltpu.make_async_copy(weights, weights_v, load_sem)
    load_weights.start()
    edges = [
        pltpu.make_async_copy(forcing.at[:, pl.ds(at, LANES)], edge_f.at[k], edge_sem.at[k])
        for k, at in enumerate((columns - LANES, 0))
    ]
    for copy in edges:
        copy.start()

    barrier = pltpu.get_barrier_semaphore()
    for side in (left, right):
        pl.semaphore_signal(barrier, inc=1, device_id=(comp, side), device_id_type=MESH)

    def greet(p, carry):
        peer = first + p
        pl.semaphore_signal(
            barrier, inc=1, device_id=(peer // doms, peer % doms), device_id_type=MESH
        )
        return carry

    lax.fori_loop(0, count, greet, 0)

    stack_left(extract[0], left_f, PAD_ROWS)
    left_b = left_f[...].astype(BF16)[:, : 3 * PAD_ROWS]

    for copy in edges:
        copy.wait()
    load(pieces - 1).wait()
    load(0).wait()
    for k, at in enumerate((columns - LANES, 0)):
        here = slice(at, at + LANES)
        edge[k, 0:levels] = state_v[:, here]
        edge[k, levels : levels + 8] = edge_f[k] * landmask[:, here].astype(F32)
        edge[k, levels + 8 : levels + 16] = jnp.broadcast_to(diffuse[:, here], (8, LANES))
        edge[k, levels + 16 : levels + 24] = jnp.broadcast_to(
            substeps[:, here].astype(F32), (8, LANES)
        )
    pl.semaphore_wait(barrier, count + 2)
    sides = [
        pltpu.make_async_remote_copy(
            src_ref=edge.at[k],
            dst_ref=halo.at[k],
            send_sem=halo_send.at[k],
            recv_sem=halo_recv.at[k],
            device_id=(comp, side),
            device_id_type=MESH,
        )
        for k, side in enumerate((right, left))
    ]
    for copy in sides:
        copy.start()

    for c in range(pieces):
        if 0 < c < pieces - 1:
            load(c).wait()

        def extract_rows(t, carry):
            for u in range(4):
                tile = c * CHUNK + t * 4 + u
                here = pl.ds(pl.multiple_of(tile * WIDE, WIDE), WIDE)
                x = jnp.concatenate(
                    [state_v[:, here], jnp.zeros((PAD_ROWS - levels, WIDE), F32)], axis=0
                )
                high, low = high_low(x)
                r = jnp.dot(
                    left_b, jnp.concatenate([high, low, high], axis=0), preferred_element_type=F32
                )
                r = r * landmask[:, here].astype(F32)
                rows_v[2 * tile] = r[:, 0:LANES]
                rows_v[2 * tile + 1] = r[:, LANES:WIDE]
            return carry

        lax.fori_loop(0, CHUNK // 4, extract_rows, 0)
    load_weights.wait()

    def split(s, carry):
        high, low = high_low(weights_v[s])
        split_w[s, 0:LANES] = high
        split_w[s, LANES:WIDE] = low
        return carry

    lax.fori_loop(0, weights_v.shape[0], split, 0)

    def send(p):
        peer = first + p
        spot = (peer // doms, peer % doms)
        return (
            pltpu.make_async_remote_copy(
                src_ref=msg.at[p],
                dst_ref=arrived.at[me],
                send_sem=msg_send.at[p],
                recv_sem=msg_recv.at[me],
                device_id=spot,
                device_id_type=MESH,
            ),
            pltpu.make_async_remote_copy(
                src_ref=tgt.at[p],
                dst_ref=targets.at[me],
                send_sem=tgt_send.at[p],
                recv_sem=tgt_recv.at[me],
                device_id=spot,
                device_id_type=MESH,
            ),
        )

    lane = lax.broadcasted_iota(jnp.int32, (1, LANES), 1)

    def group(step, carry):
        for q in range(GROUP):
            p = step * GROUP + q
            peer = first + p
            for k in range(2):
                r = rows_v[jnp.maximum(links[0, 0, peer, k], 0)]
                high = r.astype(BF16).astype(F32)
                low = r - high
                top = jnp.concatenate([high, high], axis=1)
                bottom = jnp.concatenate([low, jnp.zeros_like(low)], axis=1)
                lhs = jnp.concatenate([top, bottom], axis=0).astype(BF16)
                slot = jnp.maximum(links[2, 0, peer, k], 0)
                out = jnp.dot(lhs, split_w[slot], preferred_element_type=F32)
                msg[p, k * 8 : (k + 1) * 8] = out[0:8] + out[8:16]
            t0 = jnp.where(lane == 0, links[1, 0, peer, 0], -1)
            tgt[p] = jnp.where(lane == 1, links[1, 0, peer, 1], t0)
            for copy in send(p):
                copy.start()
        return carry

    lax.fori_loop(0, count // GROUP, group, 0)

    def finish(p, carry):
        for copy in send(p):
            copy.wait_send()
        g = first + p
        pltpu.make_async_copy(arrived.at[g], arrived.at[g], msg_recv.at[g]).wait()
        pltpu.make_async_copy(targets.at[g], targets.at[g], tgt_recv.at[g]).wait()
        return carry

    lax.fori_loop(0, count, finish, 0)
    for copy in sides:
        copy.wait()


def exchange(comps, doms, links, state, forcing, extract, diffuse, substeps, landmask, weights):
    levels, columns = state.shape
    fields = forcing.shape[0]
    slots = weights.shape[0]
    devices = comps * doms
    peers = max(doms, devices - doms)
    anywhere = pl.BlockSpec(memory_space=pl.ANY)
    vmem = pl.BlockSpec(memory_space=pltpu.VMEM)
    smem = pl.BlockSpec(memory_space=pltpu.SMEM)
    edge_rows = levels + 24
    return pl.pallas_call(
        functools.partial(exchange_kernel, comps, doms),
        out_shape=(
            jax.ShapeDtypeStruct((devices, 2 * fields, LANES), F32),
            jax.ShapeDtypeStruct((devices, 1, LANES), jnp.int32),
            jax.ShapeDtypeStruct((2, edge_rows, LANES), F32),
        ),
        in_specs=[smem, anywhere, anywhere, vmem, vmem, vmem, vmem, anywhere],
        out_specs=(anywhere, anywhere, anywhere),
        scratch_shapes=[
            pltpu.VMEM((levels, columns), F32),
            pltpu.VMEM((columns // LANES, fields, LANES), F32),
            pltpu.VMEM((2, fields, LANES), F32),
            pltpu.VMEM(weights.shape, F32),
            pltpu.VMEM((slots, WIDE, LANES), BF16),
            pltpu.VMEM((fields, WIDE), F32),
            pltpu.VMEM((peers, 2 * fields, LANES), F32),
            pltpu.VMEM((peers, 1, LANES), jnp.int32),
            pltpu.VMEM((2, edge_rows, LANES), F32),
            pltpu.SemaphoreType.DMA((columns // (CHUNK * WIDE),)),
            pltpu.SemaphoreType.DMA,
            pltpu.SemaphoreType.DMA((2,)),
            pltpu.SemaphoreType.DMA((peers,)),
            pltpu.SemaphoreType.DMA((devices,)),
            pltpu.SemaphoreType.DMA((peers,)),
            pltpu.SemaphoreType.DMA((devices,)),
            pltpu.SemaphoreType.DMA((2,)),
            pltpu.SemaphoreType.DMA((2,)),
        ],
        compiler_params=pltpu.CompilerParams(
            collective_id=0, has_side_effects=True, vmem_limit_bytes=24 << 20
        ),
        name="exchange",
    )(links, state, forcing, extract, diffuse, substeps, landmask, weights)


def advance_kernel(
    comps,
    doms,
    targets,
    state,
    forcing,
    vertical,
    inject,
    diffuse,
    substeps,
    landmask,
    arrived,
    halo,
    state_next,
    forcing_next,
    fields_v,
    out_v,
    force_v,
    next_v,
    mix_v,
    sub_v,
    left_f,
    load_sem,
    store_sem,
    next_sem,
):
    levels, columns = state.shape
    blocks = columns // WIDE
    start = LEAD // WIDE
    pieces = blocks // CHUNK
    span = CHUNK * WIDE

    def load(c):
        return pltpu.make_async_copy(
            state.at[:, pl.ds(pl.multiple_of(c * span, span), span)],
            fields_v.at[0, :, pl.ds(pl.multiple_of(c * span + LEAD, LANES), span)],
            load_sem.at[c],
        )

    def store(c):
        here = pl.ds(pl.multiple_of(c * span, span), span)
        return pltpu.make_async_copy(out_v.at[:, here], state_next.at[:, here], store_sem.at[c])

    for c in range(pieces):
        load(c).start()

    left_f[...] = jnp.zeros_like(left_f)
    high_v = (vertical[0] * DT).astype(BF16).astype(F32)
    low_v = vertical[0] * DT - high_v
    high_i = (inject[0] * DT).astype(BF16).astype(F32)
    low_i = inject[0] * DT - high_i
    for k, (v, f) in enumerate(((high_v, high_i), (high_v, high_i), (low_v, low_i))):
        at = k * PAD_ROWS
        left_f[:, at : at + levels] = v
        left_f[:, at + levels : at + PAD_ROWS] = f
    left_b = left_f[...].astype(BF16)[:, : 3 * PAD_ROWS]

    tail = LEAD + columns
    here = slice(LEAD, tail)
    force_v[:, here] = forcing[...] * landmask[...].astype(F32)
    mix_v[:, here] = diffuse[...]
    sub_v[:, here] = substeps[...]
    for k, at in enumerate((LEAD - LANES, tail)):
        there = slice(at, at + LANES)
        fields_v[0, :, there] = halo[k, 0:levels]
        force_v[:, there] = halo[k, levels : levels + 8]
        mix_v[:, there] = halo[k, levels + 8 : levels + 9]
        sub_v[:, there] = halo[k, levels + 16 : levels + 17].astype(jnp.int32)

    next_v[...] = jnp.zeros_like(next_v)
    air = (comps - 1) * doms
    is_air = lax.axis_index("comp") < comps - 1
    count = jnp.where(is_air, doms, air)
    first = jnp.where(is_air, air, 0)

    def scatter(p, carry):
        for k in range(2):
            t = targets[first + p, 0, k]
            there = pl.ds(pl.multiple_of(jnp.maximum(t, 0) * LANES, LANES), LANES)
            part = arrived[first + p, k * 8 : (k + 1) * 8]
            next_v[:, there] += jnp.where(t >= 0, part, jnp.zeros_like(part))
        return carry

    lax.fori_loop(0, count, scatter, 0)
    store_next = pltpu.make_async_copy(next_v, forcing_next, next_sem)
    store_next.start()

    lane = lax.broadcasted_iota(jnp.int32, (levels, LANES), 1)
    at_first = lane == 0
    at_last = lane == LANES - 1

    def update(j, b):
        base = b * WIDE
        if not isinstance(b, int):
            base = pl.multiple_of(base, WIDE)

        def piece(k):
            return fields_v[j, :, pl.ds(base + (k - 1) * LANES, LANES)]

        near = [piece(k) for k in range(4)]
        back = [pltpu.roll(near[k], 1, axis=1) for k in range(3)]
        ahead = [pltpu.roll(near[k], LANES - 1, axis=1) for k in range(1, 4)]
        here = pl.ds(base, WIDE)
        x = jnp.concatenate(near[1:3], axis=1)
        both = jnp.concatenate(
            [
                jnp.where(at_first, back[k], back[k + 1]) + jnp.where(at_last, ahead[k + 1], ahead[k])
                for k in range(2)
            ],
            axis=1,
        )
        high, low = high_low(jnp.concatenate([x, force_v[:, here]], axis=0))
        change = jnp.dot(
            left_b, jnp.concatenate([high, low, high], axis=0), preferred_element_type=F32
        )
        d = mix_v[:, here]
        new = (1.0 - 2.0 * d) * x + (d * both + change)
        if j > 0:
            new = jnp.where(sub_v[:, here] > j, new, x)
        if j < SUBS - 1:
            fields_v[j + 1, :, here] = new
        else:
            there = base - LEAD
            if not isinstance(b, int):
                there = pl.multiple_of(there, WIDE)
            out_v[:, pl.ds(there, WIDE)] = new

    low_b, high_b = start - 1, start + blocks

    def valid(i, j):
        b = i - 2 * j
        if j == SUBS - 1:
            return start <= b < start + blocks
        return low_b <= b <= high_b

    body_from = low_b + 2 * (SUBS - 1) + 1
    body_to = high_b + 1
    waited = 0
    last = start + blocks - 1 + 2 * (SUBS - 1)
    for i in range(low_b, body_from):
        while waited < pieces and waited * CHUNK + start <= i + 1:
            load(waited).wait()
            waited += 1
        for j in range(SUBS):
            if valid(i, j):
                update(j, i - 2 * j)

    def body(i, carry):
        coming = i + 1 - start

        @pl.when((coming % CHUNK == 0) & (coming // CHUNK >= waited) & (coming // CHUNK < pieces))
        def _():
            load(coming // CHUNK).wait()

        for j in range(SUBS):
            update(j, i - 2 * j)
        ended = i - 2 * (SUBS - 1) - start + 1

        @pl.when(ended % CHUNK == 0)
        def _():
            store(ended // CHUNK - 1).start()

        return carry

    lax.fori_loop(body_from, body_to, body, 0)
    for i in range(body_to, last + 1):
        for j in range(SUBS):
            if valid(i, j):
                update(j, i - 2 * j)
    for c in range((body_to - 1 - 2 * (SUBS - 1) - start + 1) // CHUNK, pieces):
        store(c).start()
    for c in range(pieces):
        store(c).wait()
    store_next.wait()


def advance(comps, doms, targets, state, forcing, vertical, inject, diffuse, substeps, landmask, arrived, halo):
    levels, columns = state.shape
    fields = forcing.shape[0]
    width = columns + 2 * LEAD
    pieces = columns // (CHUNK * WIDE)
    anywhere = pl.BlockSpec(memory_space=pl.ANY)
    vmem = pl.BlockSpec(memory_space=pltpu.VMEM)
    smem = pl.BlockSpec(memory_space=pltpu.SMEM)
    return pl.pallas_call(
        functools.partial(advance_kernel, comps, doms),
        out_shape=(
            jax.ShapeDtypeStruct(state.shape, F32),
            jax.ShapeDtypeStruct(forcing.shape, F32),
        ),
        in_specs=[smem, anywhere] + [vmem] * 8,
        out_specs=(anywhere, anywhere),
        scratch_shapes=[
            pltpu.VMEM((SUBS, levels, width), F32),
            pltpu.VMEM((levels, columns), F32),
            pltpu.VMEM((fields, width), F32),
            pltpu.VMEM((fields, columns), F32),
            pltpu.VMEM((1, width), F32),
            pltpu.VMEM((1, width), jnp.int32),
            pltpu.VMEM((levels, WIDE), F32),
            pltpu.SemaphoreType.DMA((pieces,)),
            pltpu.SemaphoreType.DMA((pieces,)),
            pltpu.SemaphoreType.DMA,
        ],
        compiler_params=pltpu.CompilerParams(vmem_limit_bytes=48 << 20),
        name="advance",
    )(targets, state, forcing, vertical, inject, diffuse, substeps, landmask, arrived, halo)


def solution(mesh):
    comps, doms = mesh.shape["comp"], mesh.shape["dom"]

    def local(state, forcing, vertical, inject, extract, diffuse, substeps, landmask, links, weights):
        rows = [a.reshape(1, -1) for a in (diffuse, substeps, landmask)]
        arrived, targets, halo = exchange(
            comps, doms, links, state, forcing, extract, *rows, weights
        )
        return advance(
            comps, doms, targets, state, forcing, vertical, inject, *rows, arrived, halo
        )

    return jax.shard_map(
        local,
        mesh=mesh,
        in_specs=(
            P(None, ("comp", "dom")),
            P(None, ("comp", "dom")),
            P("comp", None, None),
            P("comp", None, None),
            P("comp", None, None),
            P(("comp", "dom")),
            P(("comp", "dom")),
            P(("comp", "dom")),
            P(None, ("comp", "dom"), None, None),
            P(("comp", "dom"), None, None),
        ),
        out_specs=(P(None, ("comp", "dom")), P(None, ("comp", "dom"))),
        check_vma=False,
    )
```

```python
import functools

import jax
import jax.numpy as jnp
from jax import lax
from jax.experimental import pallas as pl
from jax.experimental.pallas import tpu as pltpu
from jax.sharding import PartitionSpec as P

SUBS = 4
DT = 0.25
LANES = 128
WIDE = 256
STRIP = 256
LEAD = 2 * STRIP
STRIPS = 2048 // STRIP
GROUP = 8
CHUNK = 8
PAD_ROWS = 80
MESH = pl.DeviceIdType.MESH
F32 = jnp.float32
BF16 = jnp.bfloat16


def high_low(x):
    high = x.astype(BF16)
    return high, (x - high.astype(F32)).astype(BF16)


def stack_left(matrix, scratch, width):
    high = matrix.astype(BF16).astype(F32)
    low = matrix - high
    scratch[...] = jnp.zeros_like(scratch)
    size = matrix.shape[1]
    scratch[:, 0:size] = high
    scratch[:, width : width + size] = high
    scratch[:, 2 * width : 2 * width + size] = low


def exchange_kernel(
    comps,
    doms,
    links,
    state,
    forcing,
    extract,
    diffuse,
    substeps,
    landmask,
    weights,
    arrived,
    targets,
    halo,
    state_v,
    rows_v,
    extract_v,
    wet_v,
    edge_f,
    edge_d,
    edge_n,
    weights_v,
    split_w,
    left_f,
    msg,
    tgt,
    edge,
    state_sem,
    load_sem,
    edge_sem,
    msg_send,
    msg_recv,
    tgt_send,
    tgt_recv,
    halo_send,
    halo_recv,
):
    levels, columns = state.shape
    comp = lax.axis_index("comp")
    dom = lax.axis_index("dom")
    me = comp * doms + dom
    air = (comps - 1) * doms
    is_air = comp < comps - 1
    count = jnp.where(is_air, doms, air)
    first = jnp.where(is_air, air, 0)
    right = lax.rem(dom + 1, doms)
    left = lax.rem(dom + doms - 1, doms)

    span = CHUNK * WIDE
    pieces = columns // span

    def load(c):
        here = pl.ds(pl.multiple_of(c * span, span), span)
        return pltpu.make_async_copy(state.at[:, here], state_v.at[:, here], state_sem.at[c])

    load(pieces - 1).start()
    for c in range(pieces - 1):
        load(c).start()
    load_weights = pltpu.make_async_copy(weights, weights_v, load_sem)
    load_weights.start()
    edges = [
        pltpu.make_async_copy(extract.at[0], extract_v, edge_sem.at[0]),
        pltpu.make_async_copy(landmask, wet_v, edge_sem.at[1]),
    ]
    for k, at in enumerate((columns - LANES, 0)):
        for m, (src, dst) in enumerate(((forcing, edge_f), (diffuse, edge_d), (substeps, edge_n))):
            edges.append(
                pltpu.make_async_copy(
                    src.at[:, pl.ds(at, LANES)], dst.at[k], edge_sem.at[2 + 3 * k + m]
                )
            )
    for copy in edges:
        copy.start()

    barrier = pltpu.get_barrier_semaphore()
    for side in (left, right):
        pl.semaphore_signal(barrier, inc=1, device_id=(comp, side), device_id_type=MESH)

    def greet(p, carry):
        peer = first + p
        pl.semaphore_signal(
            barrier, inc=1, device_id=(peer // doms, peer % doms), device_id_type=MESH
        )
        return carry

    lax.fori_loop(0, count, greet, 0)

    for copy in edges:
        copy.wait()
    stack_left(extract_v[...], left_f, PAD_ROWS)
    left_b = left_f[...].astype(BF16)[:, : 3 * PAD_ROWS]
    load(pieces - 1).wait()
    load(0).wait()
    for k, at in enumerate((columns - LANES, 0)):
        here = slice(at, at + LANES)
        edge[k, 0:levels] = state_v[:, here]
        edge[k, levels : levels + 8] = edge_f[k] * wet_v[:, here].astype(F32)
        edge[k, levels + 8 : levels + 16] = jnp.broadcast_to(edge_d[k], (8, LANES))
        edge[k, levels + 16 : levels + 24] = jnp.broadcast_to(
            edge_n[k].astype(F32), (8, LANES)
        )
    pl.semaphore_wait(barrier, count + 2)
    sides = [
        pltpu.make_async_remote_copy(
            src_ref=edge.at[k],
            dst_ref=halo.at[k],
            send_sem=halo_send.at[k],
            recv_sem=halo_recv.at[k],
            device_id=(comp, side),
            device_id_type=MESH,
        )
        for k, side in enumerate((right, left))
    ]
    for copy in sides:
        copy.start()

    for c in range(pieces):
        if 0 < c < pieces - 1:
            load(c).wait()

        outs = []
        for u in range(CHUNK):
            here = pl.ds((c * CHUNK + u) * WIDE, WIDE)
            x = jnp.concatenate(
                [state_v[:, here], jnp.zeros((PAD_ROWS - levels, WIDE), F32)], axis=0
            )
            high, low = high_low(x)
            r = jnp.dot(
                left_b, jnp.concatenate([high, low, high], axis=0), preferred_element_type=F32
            )
            outs.append(r * wet_v[:, here].astype(F32))
        for u in range(CHUNK):
            tile = c * CHUNK + u
            rows_v[2 * tile] = outs[u][:, 0:LANES]
            rows_v[2 * tile + 1] = outs[u][:, LANES:WIDE]
    load_weights.wait()

    def split(s, carry):
        high, low = high_low(weights_v[s])
        split_w[s, 0:LANES] = high
        split_w[s, LANES:WIDE] = low
        return carry

    lax.fori_loop(0, weights_v.shape[0], split, 0, unroll=4)

    def send(p):
        peer = first + p
        spot = (peer // doms, peer % doms)
        return (
            pltpu.make_async_remote_copy(
                src_ref=msg.at[p],
                dst_ref=arrived.at[me],
                send_sem=msg_send.at[p],
                recv_sem=msg_recv.at[me],
                device_id=spot,
                device_id_type=MESH,
            ),
            pltpu.make_async_remote_copy(
                src_ref=tgt.at[p],
                dst_ref=targets.at[me],
                send_sem=tgt_send.at[p],
                recv_sem=tgt_recv.at[me],
                device_id=spot,
                device_id_type=MESH,
            ),
        )

    lane = lax.broadcasted_iota(jnp.int32, (1, LANES), 1)

    def group(step, carry):
        outs = []
        for q in range(GROUP):
            peer = first + step * GROUP + q
            for k in range(2):
                r = rows_v[jnp.maximum(links[0, 0, k, peer], 0)]
                high = r.astype(BF16).astype(F32)
                low = r - high
                top = jnp.concatenate([high, high], axis=1)
                bottom = jnp.concatenate([low, jnp.zeros_like(low)], axis=1)
                lhs = jnp.concatenate([top, bottom], axis=0).astype(BF16)
                slot = jnp.maximum(links[2, 0, k, peer], 0)
                out = jnp.dot(lhs, split_w[slot], preferred_element_type=F32)
                outs.append(out[0:8] + out[8:16])
        for q in range(GROUP):
            p = step * GROUP + q
            peer = first + p
            msg[p] = jnp.concatenate(outs[2 * q : 2 * q + 2], axis=0)
            t0 = jnp.where(lane == 0, links[1, 0, 0, peer], -1)
            tgt[p] = jnp.where(lane == 1, links[1, 0, 1, peer], t0)
        for q in range(GROUP):
            for copy in send(step * GROUP + q):
                copy.start()
        return carry

    lax.fori_loop(0, count // GROUP, group, 0)

    def finish(p, carry):
        for copy in send(p):
            copy.wait_send()
        g = first + p
        pltpu.make_async_copy(arrived.at[g], arrived.at[g], msg_recv.at[g]).wait()
        pltpu.make_async_copy(targets.at[g], targets.at[g], tgt_recv.at[g]).wait()
        return carry

    lax.fori_loop(0, count, finish, 0)
    for copy in sides:
        copy.wait()


def exchange(comps, doms, links, state, forcing, extract, diffuse, substeps, landmask, weights):
    levels, columns = state.shape
    fields = forcing.shape[0]
    slots = weights.shape[0]
    devices = comps * doms
    peers = max(doms, devices - doms)
    hbm = pl.BlockSpec(memory_space=pltpu.HBM)
    smem = pl.BlockSpec(memory_space=pltpu.SMEM)
    edge_rows = levels + 24
    return pl.pallas_call(
        functools.partial(exchange_kernel, comps, doms),
        out_shape=(
            jax.ShapeDtypeStruct((devices, 2 * fields, LANES), F32),
            jax.ShapeDtypeStruct((devices, 1, LANES), jnp.int32),
            jax.ShapeDtypeStruct((2, edge_rows, LANES), F32),
        ),
        in_specs=[smem] + [hbm] * 7,
        out_specs=(hbm, hbm, hbm),
        scratch_shapes=[
            pltpu.VMEM((levels, columns), F32),
            pltpu.VMEM((columns // LANES, fields, LANES), F32),
            pltpu.VMEM((fields, levels), F32),
            pltpu.VMEM((1, columns), jnp.int32),
            pltpu.VMEM((2, fields, LANES), F32),
            pltpu.VMEM((2, 1, LANES), F32),
            pltpu.VMEM((2, 1, LANES), jnp.int32),
            pltpu.VMEM(weights.shape, F32),
            pltpu.VMEM((slots, WIDE, LANES), BF16),
            pltpu.VMEM((fields, WIDE), F32),
            pltpu.VMEM((peers, 2 * fields, LANES), F32),
            pltpu.VMEM((peers, 1, LANES), jnp.int32),
            pltpu.VMEM((2, edge_rows, LANES), F32),
            pltpu.SemaphoreType.DMA((columns // (CHUNK * WIDE),)),
            pltpu.SemaphoreType.DMA,
            pltpu.SemaphoreType.DMA((8,)),
            pltpu.SemaphoreType.DMA((peers,)),
            pltpu.SemaphoreType.DMA((devices,)),
            pltpu.SemaphoreType.DMA((peers,)),
            pltpu.SemaphoreType.DMA((devices,)),
            pltpu.SemaphoreType.DMA((2,)),
            pltpu.SemaphoreType.DMA((2,)),
        ],
        compiler_params=pltpu.CompilerParams(
            collective_id=0, has_side_effects=True, vmem_limit_bytes=60 << 20
        ),
        name="exchange",
    )(links, state, forcing, extract, diffuse, substeps, landmask, weights)


def advance_kernel(
    comps,
    doms,
    targets,
    state,
    forcing,
    vertical,
    inject,
    diffuse,
    substeps,
    landmask,
    arrived,
    halo,
    state_next,
    forcing_next,
    field_0,
    field_1,
    field_2,
    field_3,
    out_v,
    force_v,
    next_v,
    mix_v,
    sub_v,
    wet_v,
    vertical_v,
    inject_v,
    arrived_v,
    halo_v,
    left_f,
    load_sem,
    store_sem,
    next_sem,
    small_sem,
):
    levels, columns = state.shape
    chain = (field_0, field_1, field_2, field_3)
    blocks = columns // STRIP
    start = LEAD // STRIP
    pieces = blocks // STRIPS
    span = STRIPS * STRIP

    def load(c):
        return pltpu.make_async_copy(
            state.at[:, pl.ds(pl.multiple_of(c * span, span), span)],
            field_0.at[:, pl.ds(pl.multiple_of(c * span + LEAD, LANES), span)],
            load_sem.at[c],
        )

    def store(c):
        here = pl.ds(pl.multiple_of(c * span, span), span)
        return pltpu.make_async_copy(out_v.at[:, here], state_next.at[:, here], store_sem.at[c])

    tail = LEAD + columns
    here = slice(LEAD, tail)
    small = [
        pltpu.make_async_copy(src, dst, small_sem.at[k])
        for k, (src, dst) in enumerate(
            (
                (vertical.at[0], vertical_v),
                (inject.at[0], inject_v),
                (halo, halo_v),
                (diffuse, mix_v.at[:, pl.ds(LEAD, columns)]),
                (substeps, sub_v.at[:, pl.ds(LEAD, columns)]),
                (landmask, wet_v),
                (forcing, force_v.at[:, pl.ds(LEAD, columns)]),
                (arrived, arrived_v),
            )
        )
    ]
    for copy in small[:3]:
        copy.start()
    load(0).start()
    for copy in small[3:]:
        copy.start()
    for c in range(1, pieces):
        load(c).start()
    next_v[...] = jnp.zeros_like(next_v)
    left_f[...] = jnp.zeros_like(left_f)
    for copy in small:
        copy.wait()
    high_v = (vertical_v[...] * DT).astype(BF16).astype(F32)
    low_v = vertical_v[...] * DT - high_v
    inject_t = jnp.transpose(inject_v[...])[0:levels] * DT
    high_i = inject_t.astype(BF16).astype(F32)
    low_i = inject_t - high_i
    for k, (v, f) in enumerate(((high_v, high_i), (high_v, high_i), (low_v, low_i))):
        at = k * PAD_ROWS
        left_f[:, at : at + levels] = v
        left_f[:, at + levels : at + PAD_ROWS] = f
    left_b = left_f[...].astype(BF16)[:, : 3 * PAD_ROWS]

    force_v[:, here] = force_v[:, here] * wet_v[...].astype(F32)
    for k, at in enumerate((LEAD - LANES, tail)):
        there = slice(at, at + LANES)
        field_0[:, there] = halo_v[k, 0:levels]
        force_v[:, there] = halo_v[k, levels : levels + 8]
        mix_v[:, there] = halo_v[k, levels + 8 : levels + 9]
        sub_v[:, there] = halo_v[k, levels + 16 : levels + 17].astype(jnp.int32)

    air = (comps - 1) * doms
    is_air = lax.axis_index("comp") < comps - 1
    count = jnp.where(is_air, doms, air)
    first = jnp.where(is_air, air, 0)

    def scatter(p, carry):
        for k in range(2):
            t = targets[first + p, 0, k]
            there = pl.ds(pl.multiple_of(jnp.maximum(t, 0) * LANES, LANES), LANES)
            part = arrived_v[first + p, k * 8 : (k + 1) * 8]
            next_v[:, there] += jnp.where(t >= 0, part, jnp.zeros_like(part))
        return carry

    lax.fori_loop(0, count, scatter, 0)
    store_next = pltpu.make_async_copy(next_v, forcing_next, next_sem)
    store_next.start()

    lane = lax.broadcasted_iota(jnp.int32, (levels, LANES), 1)
    at_first = lane == 0
    at_last = lane == LANES - 1

    def compute(j, b):
        base = b * STRIP
        if not isinstance(b, int):
            base = pl.multiple_of(base, STRIP)

        def piece(k):
            return chain[j][:, pl.ds(base + (k - 1) * LANES, LANES)]

        near = [piece(k) for k in range(4)]
        back = [pltpu.roll(near[k], 1, axis=1) for k in range(3)]
        ahead = [pltpu.roll(near[k], LANES - 1, axis=1) for k in range(1, 4)]
        here = pl.ds(base, STRIP)
        x = jnp.concatenate(near[1:3], axis=1)
        both = jnp.concatenate(
            [
                jnp.where(at_first, back[k], back[k + 1]) + jnp.where(at_last, ahead[k + 1], ahead[k])
                for k in range(2)
            ],
            axis=1,
        )
        high, low = high_low(jnp.concatenate([x, force_v[:, here]], axis=0))
        change = jnp.dot(
            left_b, jnp.concatenate([high, low, high], axis=0), preferred_element_type=F32
        )
        d = mix_v[:, here]
        new = (1.0 - 2.0 * d) * x + (d * both + change)
        if j > 0:
            new = jnp.where(sub_v[:, here] > j, new, x)
        return new

    def keep(j, b, new):
        base = b * STRIP
        if not isinstance(b, int):
            base = pl.multiple_of(base, STRIP)
        if j < SUBS - 1:
            chain[j + 1][:, pl.ds(base, STRIP)] = new
        else:
            there = base - LEAD
            if not isinstance(b, int):
                there = pl.multiple_of(there, STRIP)
            out_v[:, pl.ds(there, STRIP)] = new

    def advance_all(i, subs):
        for j in reversed(subs):
            keep(j, i - 2 * j, compute(j, i - 2 * j))

    low_b, high_b = start - 1, start + blocks

    def valid(i, j):
        b = i - 2 * j
        if j == SUBS - 1:
            return start <= b < start + blocks
        return low_b <= b <= high_b

    body_from = low_b + 2 * (SUBS - 1) + 1
    body_to = high_b + 1
    waited = 0
    last = start + blocks - 1 + 2 * (SUBS - 1)
    for i in range(low_b, body_from):
        while waited < pieces and waited * STRIPS + start <= i + 1:
            load(waited).wait()
            waited += 1
        advance_all(i, [j for j in range(SUBS) if valid(i, j)])

    def body(i, carry):
        coming = i + 1 - start

        @pl.when((coming % STRIPS == 0) & (coming // STRIPS >= waited) & (coming // STRIPS < pieces))
        def _():
            load(coming // STRIPS).wait()

        advance_all(i, list(range(SUBS)))
        ended = i - 2 * (SUBS - 1) - start + 1

        @pl.when(ended % STRIPS == 0)
        def _():
            store(ended // STRIPS - 1).start()

        return carry

    lax.fori_loop(body_from, body_to, body, 0)
    for i in range(body_to, last + 1):
        advance_all(i, [j for j in range(SUBS) if valid(i, j)])
    for c in range((body_to - 1 - 2 * (SUBS - 1) - start + 1) // STRIPS, pieces):
        store(c).start()
    for c in range(pieces):
        store(c).wait()
    store_next.wait()


def advance(comps, doms, targets, state, forcing, vertical, inject, diffuse, substeps, landmask, arrived, halo):
    levels, columns = state.shape
    fields = forcing.shape[0]
    width = columns + 2 * LEAD
    pieces = columns // (STRIPS * STRIP)
    hbm = pl.BlockSpec(memory_space=pltpu.HBM)
    smem = pl.BlockSpec(memory_space=pltpu.SMEM)
    return pl.pallas_call(
        functools.partial(advance_kernel, comps, doms),
        out_shape=(
            jax.ShapeDtypeStruct(state.shape, F32),
            jax.ShapeDtypeStruct(forcing.shape, F32),
        ),
        in_specs=[smem] + [hbm] * 9,
        out_specs=(hbm, hbm),
        scratch_shapes=[
            pltpu.VMEM((levels, width), F32),
            pltpu.VMEM((levels, width), F32),
            pltpu.VMEM((levels, width), F32),
            pltpu.VMEM((levels, width), F32),
            pltpu.VMEM((levels, columns), F32),
            pltpu.VMEM((fields, width), F32),
            pltpu.VMEM((fields, columns), F32),
            pltpu.VMEM((1, width), F32),
            pltpu.VMEM((1, width), jnp.int32),
            pltpu.VMEM((1, columns), jnp.int32),
            pltpu.VMEM((levels, levels), F32),
            pltpu.VMEM((fields, levels), F32),
            pltpu.VMEM(arrived.shape, F32),
            pltpu.VMEM(halo.shape, F32),
            pltpu.VMEM((levels, STRIP), F32),
            pltpu.SemaphoreType.DMA((pieces,)),
            pltpu.SemaphoreType.DMA((pieces,)),
            pltpu.SemaphoreType.DMA,
            pltpu.SemaphoreType.DMA((8,)),
        ],
        compiler_params=pltpu.CompilerParams(vmem_limit_bytes=60 << 20),
        name="advance",
    )(targets, state, forcing, vertical, inject, diffuse, substeps, landmask, arrived, halo)


def solution(mesh):
    comps, doms = mesh.shape["comp"], mesh.shape["dom"]

    def local(state, forcing, vertical, inject, extract, diffuse, substeps, landmask, links, weights):
        rows = [a.reshape(1, -1) for a in (diffuse, substeps, landmask)]
        arrived, targets, halo = exchange(
            comps, doms, links.swapaxes(2, 3), state, forcing, extract, *rows, weights
        )
        return advance(
            comps, doms, targets, state, forcing, vertical, inject.swapaxes(1, 2), *rows, arrived, halo
        )

    return jax.shard_map(
        local,
        mesh=mesh,
        in_specs=(
            P(None, ("comp", "dom")),
            P(None, ("comp", "dom")),
            P("comp", None, None),
            P("comp", None, None),
            P("comp", None, None),
            P(("comp", "dom")),
            P(("comp", "dom")),
            P(("comp", "dom")),
            P(None, ("comp", "dom"), None, None),
            P(("comp", "dom"), None, None),
        ),
        out_specs=(P(None, ("comp", "dom")), P(None, ("comp", "dom"))),
        check_vma=False,
    )
```

```python
import functools

import jax
import jax.numpy as jnp
from jax import lax
from jax.experimental import pallas as pl
from jax.experimental.pallas import tpu as pltpu
from jax.sharding import PartitionSpec as P

SUBS = 4
DT = 0.25
LANES = 128
WIDE = 256
STRIP = 512
LEAD = 2 * STRIP
STRIPS = 2048 // STRIP
GROUP = 8
CHUNK = 8
PAD_ROWS = 80
MESH = pl.DeviceIdType.MESH
F32 = jnp.float32
BF16 = jnp.bfloat16


def high_low(x):
    high = x.astype(BF16)
    return high, (x - high.astype(F32)).astype(BF16)


def stack_left(matrix, scratch, width):
    high = matrix.astype(BF16).astype(F32)
    low = matrix - high
    scratch[...] = jnp.zeros_like(scratch)
    size = matrix.shape[1]
    scratch[:, 0:size] = high
    scratch[:, width : width + size] = high
    scratch[:, 2 * width : 2 * width + size] = low


def exchange_kernel(
    comps,
    doms,
    links,
    state,
    forcing,
    extract,
    diffuse,
    substeps,
    landmask,
    weights,
    arrived,
    targets,
    halo,
    state_v,
    rows_v,
    extract_v,
    wet_v,
    edge_f,
    edge_d,
    edge_n,
    weights_v,
    split_w,
    left_f,
    msg,
    tgt,
    edge,
    state_sem,
    load_sem,
    edge_sem,
    msg_send,
    msg_recv,
    tgt_send,
    tgt_recv,
    halo_send,
    halo_recv,
):
    levels, columns = state.shape
    comp = lax.axis_index("comp")
    dom = lax.axis_index("dom")
    me = comp * doms + dom
    air = (comps - 1) * doms
    is_air = comp < comps - 1
    count = jnp.where(is_air, doms, air)
    first = jnp.where(is_air, air, 0)
    right = lax.rem(dom + 1, doms)
    left = lax.rem(dom + doms - 1, doms)

    span = CHUNK * WIDE
    pieces = columns // span

    def load(c):
        here = pl.ds(pl.multiple_of(c * span, span), span)
        return pltpu.make_async_copy(state.at[:, here], state_v.at[:, here], state_sem.at[c])

    load(pieces - 1).start()
    for c in range(pieces - 1):
        load(c).start()
    load_weights = pltpu.make_async_copy(weights, weights_v, load_sem)
    load_weights.start()
    edges = [
        pltpu.make_async_copy(extract.at[0], extract_v, edge_sem.at[0]),
        pltpu.make_async_copy(landmask, wet_v, edge_sem.at[1]),
    ]
    for k, at in enumerate((columns - LANES, 0)):
        for m, (src, dst) in enumerate(((forcing, edge_f), (diffuse, edge_d), (substeps, edge_n))):
            edges.append(
                pltpu.make_async_copy(
                    src.at[:, pl.ds(at, LANES)], dst.at[k], edge_sem.at[2 + 3 * k + m]
                )
            )
    for copy in edges:
        copy.start()

    barrier = pltpu.get_barrier_semaphore()
    for side in (left, right):
        pl.semaphore_signal(barrier, inc=1, device_id=(comp, side), device_id_type=MESH)

    def greet(p, carry):
        peer = first + p
        pl.semaphore_signal(
            barrier, inc=1, device_id=(peer // doms, peer % doms), device_id_type=MESH
        )
        return carry

    lax.fori_loop(0, count, greet, 0)

    for copy in edges:
        copy.wait()
    stack_left(extract_v[...], left_f, PAD_ROWS)
    left_b = left_f[...].astype(BF16)[:, : 3 * PAD_ROWS]
    load(pieces - 1).wait()
    load(0).wait()
    for k, at in enumerate((columns - LANES, 0)):
        here = slice(at, at + LANES)
        edge[k, 0:levels] = state_v[:, here]
        edge[k, levels : levels + 8] = edge_f[k] * wet_v[:, here].astype(F32)
        edge[k, levels + 8 : levels + 16] = jnp.broadcast_to(edge_d[k], (8, LANES))
        edge[k, levels + 16 : levels + 24] = jnp.broadcast_to(
            edge_n[k].astype(F32), (8, LANES)
        )
    pl.semaphore_wait(barrier, count + 2)
    sides = [
        pltpu.make_async_remote_copy(
            src_ref=edge.at[k],
            dst_ref=halo.at[k],
            send_sem=halo_send.at[k],
            recv_sem=halo_recv.at[k],
            device_id=(comp, side),
            device_id_type=MESH,
        )
        for k, side in enumerate((right, left))
    ]
    for copy in sides:
        copy.start()

    for c in range(pieces):
        if 0 < c < pieces - 1:
            load(c).wait()

        outs = []
        for u in range(CHUNK):
            here = pl.ds((c * CHUNK + u) * WIDE, WIDE)
            x = jnp.concatenate(
                [state_v[:, here], jnp.zeros((PAD_ROWS - levels, WIDE), F32)], axis=0
            )
            high, low = high_low(x)
            r = jnp.dot(
                left_b, jnp.concatenate([high, low, high], axis=0), preferred_element_type=F32
            )
            outs.append(r * wet_v[:, here].astype(F32))
        for u in range(CHUNK):
            tile = c * CHUNK + u
            rows_v[2 * tile] = outs[u][:, 0:LANES]
            rows_v[2 * tile + 1] = outs[u][:, LANES:WIDE]
    load_weights.wait()

    def split(s, carry):
        high, low = high_low(weights_v[s])
        split_w[s, 0:LANES] = high
        split_w[s, LANES:WIDE] = low
        return carry

    lax.fori_loop(0, weights_v.shape[0], split, 0, unroll=4)

    def send(p):
        peer = first + p
        spot = (peer // doms, peer % doms)
        return (
            pltpu.make_async_remote_copy(
                src_ref=msg.at[p],
                dst_ref=arrived.at[me],
                send_sem=msg_send.at[p],
                recv_sem=msg_recv.at[me],
                device_id=spot,
                device_id_type=MESH,
            ),
            pltpu.make_async_remote_copy(
                src_ref=tgt.at[p],
                dst_ref=targets.at[me],
                send_sem=tgt_send.at[p],
                recv_sem=tgt_recv.at[me],
                device_id=spot,
                device_id_type=MESH,
            ),
        )

    lane = lax.broadcasted_iota(jnp.int32, (1, LANES), 1)

    def group(step, carry):
        outs = []
        for q in range(GROUP):
            peer = first + step * GROUP + q
            for k in range(2):
                r = rows_v[jnp.maximum(links[0, 0, k, peer], 0)]
                high = r.astype(BF16).astype(F32)
                low = r - high
                top = jnp.concatenate([high, high], axis=1)
                bottom = jnp.concatenate([low, jnp.zeros_like(low)], axis=1)
                lhs = jnp.concatenate([top, bottom], axis=0).astype(BF16)
                slot = jnp.maximum(links[2, 0, k, peer], 0)
                out = jnp.dot(lhs, split_w[slot], preferred_element_type=F32)
                outs.append(out[0:8] + out[8:16])
        for q in range(GROUP):
            p = step * GROUP + q
            peer = first + p
            msg[p] = jnp.concatenate(outs[2 * q : 2 * q + 2], axis=0)
            t0 = jnp.where(lane == 0, links[1, 0, 0, peer], -1)
            tgt[p] = jnp.where(lane == 1, links[1, 0, 1, peer], t0)
        for q in range(GROUP):
            for copy in send(step * GROUP + q):
                copy.start()
        return carry

    lax.fori_loop(0, count // GROUP, group, 0)

    def finish(p, carry):
        for copy in send(p):
            copy.wait_send()
        g = first + p
        pltpu.make_async_copy(arrived.at[g], arrived.at[g], msg_recv.at[g]).wait()
        pltpu.make_async_copy(targets.at[g], targets.at[g], tgt_recv.at[g]).wait()
        return carry

    lax.fori_loop(0, count, finish, 0)
    for copy in sides:
        copy.wait()


def exchange(comps, doms, links, state, forcing, extract, diffuse, substeps, landmask, weights):
    levels, columns = state.shape
    fields = forcing.shape[0]
    slots = weights.shape[0]
    devices = comps * doms
    peers = max(doms, devices - doms)
    hbm = pl.BlockSpec(memory_space=pltpu.HBM)
    smem = pl.BlockSpec(memory_space=pltpu.SMEM)
    edge_rows = levels + 24
    return pl.pallas_call(
        functools.partial(exchange_kernel, comps, doms),
        out_shape=(
            jax.ShapeDtypeStruct((devices, 2 * fields, LANES), F32),
            jax.ShapeDtypeStruct((devices, 1, LANES), jnp.int32),
            jax.ShapeDtypeStruct((2, edge_rows, LANES), F32),
        ),
        in_specs=[smem] + [hbm] * 7,
        out_specs=(hbm, hbm, hbm),
        scratch_shapes=[
            pltpu.VMEM((levels, columns), F32),
            pltpu.VMEM((columns // LANES, fields, LANES), F32),
            pltpu.VMEM((fields, levels), F32),
            pltpu.VMEM((1, columns), jnp.int32),
            pltpu.VMEM((2, fields, LANES), F32),
            pltpu.VMEM((2, 1, LANES), F32),
            pltpu.VMEM((2, 1, LANES), jnp.int32),
            pltpu.VMEM(weights.shape, F32),
            pltpu.VMEM((slots, WIDE, LANES), BF16),
            pltpu.VMEM((fields, WIDE), F32),
            pltpu.VMEM((peers, 2 * fields, LANES), F32),
            pltpu.VMEM((peers, 1, LANES), jnp.int32),
            pltpu.VMEM((2, edge_rows, LANES), F32),
            pltpu.SemaphoreType.DMA((columns // (CHUNK * WIDE),)),
            pltpu.SemaphoreType.DMA,
            pltpu.SemaphoreType.DMA((8,)),
            pltpu.SemaphoreType.DMA((peers,)),
            pltpu.SemaphoreType.DMA((devices,)),
            pltpu.SemaphoreType.DMA((peers,)),
            pltpu.SemaphoreType.DMA((devices,)),
            pltpu.SemaphoreType.DMA((2,)),
            pltpu.SemaphoreType.DMA((2,)),
        ],
        compiler_params=pltpu.CompilerParams(
            collective_id=0, has_side_effects=True, vmem_limit_bytes=60 << 20
        ),
        name="exchange",
    )(links, state, forcing, extract, diffuse, substeps, landmask, weights)


def advance_kernel(
    comps,
    doms,
    targets,
    state,
    forcing,
    vertical,
    inject,
    diffuse,
    substeps,
    landmask,
    arrived,
    halo,
    state_next,
    forcing_next,
    field_0,
    field_1,
    field_2,
    field_3,
    out_v,
    force_v,
    next_v,
    mix_v,
    sub_v,
    wet_v,
    vertical_v,
    inject_v,
    arrived_v,
    halo_v,
    left_f,
    load_sem,
    store_sem,
    next_sem,
    small_sem,
):
    levels, columns = state.shape
    chain = (field_0, field_1, field_2, field_3)
    blocks = columns // STRIP
    start = LEAD // STRIP
    pieces = blocks // STRIPS
    span = STRIPS * STRIP

    def load(c):
        return pltpu.make_async_copy(
            state.at[:, pl.ds(pl.multiple_of(c * span, span), span)],
            field_0.at[:, pl.ds(pl.multiple_of(c * span + LEAD, LANES), span)],
            load_sem.at[c],
        )

    def store(c):
        here = pl.ds(pl.multiple_of(c * span, span), span)
        return pltpu.make_async_copy(out_v.at[:, here], state_next.at[:, here], store_sem.at[c])

    tail = LEAD + columns
    here = slice(LEAD, tail)
    small = [
        pltpu.make_async_copy(src, dst, small_sem.at[k])
        for k, (src, dst) in enumerate(
            (
                (vertical.at[0], vertical_v),
                (inject.at[0], inject_v),
                (halo, halo_v),
                (diffuse, mix_v.at[:, pl.ds(LEAD, columns)]),
                (substeps, sub_v.at[:, pl.ds(LEAD, columns)]),
                (landmask, wet_v),
                (forcing, force_v.at[:, pl.ds(LEAD, columns)]),
                (arrived, arrived_v),
            )
        )
    ]
    for copy in small[:3]:
        copy.start()
    load(0).start()
    for copy in small[3:]:
        copy.start()
    for c in range(1, pieces):
        load(c).start()
    next_v[...] = jnp.zeros_like(next_v)
    left_f[...] = jnp.zeros_like(left_f)
    for copy in small:
        copy.wait()
    high_v = (vertical_v[...] * DT).astype(BF16).astype(F32)
    low_v = vertical_v[...] * DT - high_v
    inject_t = jnp.transpose(inject_v[...])[0:levels] * DT
    high_i = inject_t.astype(BF16).astype(F32)
    low_i = inject_t - high_i
    for k, (v, f) in enumerate(((high_v, high_i), (high_v, high_i), (low_v, low_i))):
        at = k * PAD_ROWS
        left_f[:, at : at + levels] = v
        left_f[:, at + levels : at + PAD_ROWS] = f
    left_b = left_f[...].astype(BF16)[:, : 3 * PAD_ROWS]

    force_v[:, here] = force_v[:, here] * wet_v[...].astype(F32)
    for k, at in enumerate((LEAD - LANES, tail)):
        there = slice(at, at + LANES)
        field_0[:, there] = halo_v[k, 0:levels]
        force_v[:, there] = halo_v[k, levels : levels + 8]
        mix_v[:, there] = halo_v[k, levels + 8 : levels + 9]
        sub_v[:, there] = halo_v[k, levels + 16 : levels + 17].astype(jnp.int32)

    air = (comps - 1) * doms
    is_air = lax.axis_index("comp") < comps - 1
    count = jnp.where(is_air, doms, air)
    first = jnp.where(is_air, air, 0)

    def scatter(p, carry):
        for k in range(2):
            t = targets[first + p, 0, k]
            there = pl.ds(pl.multiple_of(jnp.maximum(t, 0) * LANES, LANES), LANES)
            part = arrived_v[first + p, k * 8 : (k + 1) * 8]
            next_v[:, there] += jnp.where(t >= 0, part, jnp.zeros_like(part))
        return carry

    lax.fori_loop(0, count, scatter, 0)
    store_next = pltpu.make_async_copy(next_v, forcing_next, next_sem)
    store_next.start()

    lane = lax.broadcasted_iota(jnp.int32, (levels, LANES), 1)
    at_first = lane == 0
    at_last = lane == LANES - 1

    def compute(j, b):
        base = b * STRIP
        if not isinstance(b, int):
            base = pl.multiple_of(base, STRIP)

        def piece(k):
            return chain[j][:, pl.ds(base + (k - 1) * LANES, LANES)]

        here = pl.ds(base, STRIP)
        x = chain[j][:, here]
        near = chain[j][:, pl.ds(base - LANES, STRIP + 2 * LANES)]
        both = (pltpu.roll(near, 1, axis=1) + pltpu.roll(near, STRIP + 2 * LANES - 1, axis=1))[
            :, LANES : LANES + STRIP
        ]
        high, low = high_low(jnp.concatenate([x, force_v[:, here]], axis=0))
        change = jnp.dot(
            left_b, jnp.concatenate([high, low, high], axis=0), preferred_element_type=F32
        )
        d = mix_v[:, here]
        new = (1.0 - 2.0 * d) * x + (d * both + change)
        if j > 0:
            new = jnp.where(sub_v[:, here] > j, new, x)
        return new

    def keep(j, b, new):
        base = b * STRIP
        if not isinstance(b, int):
            base = pl.multiple_of(base, STRIP)
        if j < SUBS - 1:
            chain[j + 1][:, pl.ds(base, STRIP)] = new
        else:
            there = base - LEAD
            if not isinstance(b, int):
                there = pl.multiple_of(there, STRIP)
            out_v[:, pl.ds(there, STRIP)] = new

    def advance_all(i, subs):
        for j in reversed(subs):
            keep(j, i - 2 * j, compute(j, i - 2 * j))

    low_b, high_b = start - 1, start + blocks

    def valid(i, j):
        b = i - 2 * j
        if j == SUBS - 1:
            return start <= b < start + blocks
        return low_b <= b <= high_b

    body_from = low_b + 2 * (SUBS - 1) + 1
    body_to = high_b + 1
    waited = 0
    last = start + blocks - 1 + 2 * (SUBS - 1)
    for i in range(low_b, body_from):
        while waited < pieces and waited * STRIPS + start <= i + 1:
            load(waited).wait()
            waited += 1
        advance_all(i, [j for j in range(SUBS) if valid(i, j)])

    def body(i, carry):
        coming = i + 1 - start

        @pl.when((coming % STRIPS == 0) & (coming // STRIPS >= waited) & (coming // STRIPS < pieces))
        def _():
            load(coming // STRIPS).wait()

        advance_all(i, list(range(SUBS)))
        ended = i - 2 * (SUBS - 1) - start + 1

        @pl.when(ended % STRIPS == 0)
        def _():
            store(ended // STRIPS - 1).start()

        return carry

    lax.fori_loop(body_from, body_to, body, 0)
    for i in range(body_to, last + 1):
        advance_all(i, [j for j in range(SUBS) if valid(i, j)])
    for c in range((body_to - 1 - 2 * (SUBS - 1) - start + 1) // STRIPS, pieces):
        store(c).start()
    for c in range(pieces):
        store(c).wait()
    store_next.wait()


def advance(comps, doms, targets, state, forcing, vertical, inject, diffuse, substeps, landmask, arrived, halo):
    levels, columns = state.shape
    fields = forcing.shape[0]
    width = columns + 2 * LEAD
    pieces = columns // (STRIPS * STRIP)
    hbm = pl.BlockSpec(memory_space=pltpu.HBM)
    smem = pl.BlockSpec(memory_space=pltpu.SMEM)
    return pl.pallas_call(
        functools.partial(advance_kernel, comps, doms),
        out_shape=(
            jax.ShapeDtypeStruct(state.shape, F32),
            jax.ShapeDtypeStruct(forcing.shape, F32),
        ),
        in_specs=[smem] + [hbm] * 9,
        out_specs=(hbm, hbm),
        scratch_shapes=[
            pltpu.VMEM((levels, width), F32),
            pltpu.VMEM((levels, width), F32),
            pltpu.VMEM((levels, width), F32),
            pltpu.VMEM((levels, width), F32),
            pltpu.VMEM((levels, columns), F32),
            pltpu.VMEM((fields, width), F32),
            pltpu.VMEM((fields, columns), F32),
            pltpu.VMEM((1, width), F32),
            pltpu.VMEM((1, width), jnp.int32),
            pltpu.VMEM((1, columns), jnp.int32),
            pltpu.VMEM((levels, levels), F32),
            pltpu.VMEM((fields, levels), F32),
            pltpu.VMEM(arrived.shape, F32),
            pltpu.VMEM(halo.shape, F32),
            pltpu.VMEM((levels, WIDE), F32),
            pltpu.SemaphoreType.DMA((pieces,)),
            pltpu.SemaphoreType.DMA((pieces,)),
            pltpu.SemaphoreType.DMA,
            pltpu.SemaphoreType.DMA((8,)),
        ],
        compiler_params=pltpu.CompilerParams(vmem_limit_bytes=60 << 20),
        name="advance",
    )(targets, state, forcing, vertical, inject, diffuse, substeps, landmask, arrived, halo)


def solution(mesh):
    comps, doms = mesh.shape["comp"], mesh.shape["dom"]

    def local(state, forcing, vertical, inject, extract, diffuse, substeps, landmask, links, weights):
        rows = [a.reshape(1, -1) for a in (diffuse, substeps, landmask)]
        arrived, targets, halo = exchange(
            comps, doms, links.swapaxes(2, 3), state, forcing, extract, *rows, weights
        )
        return advance(
            comps, doms, targets, state, forcing, vertical, inject.swapaxes(1, 2), *rows, arrived, halo
        )

    return jax.shard_map(
        local,
        mesh=mesh,
        in_specs=(
            P(None, ("comp", "dom")),
            P(None, ("comp", "dom")),
            P("comp", None, None),
            P("comp", None, None),
            P("comp", None, None),
            P(("comp", "dom")),
            P(("comp", "dom")),
            P(("comp", "dom")),
            P(None, ("comp", "dom"), None, None),
            P(("comp", "dom"), None, None),
        ),
        out_specs=(P(None, ("comp", "dom")), P(None, ("comp", "dom"))),
        check_vma=False,
    )
```
